32 devices in a mesh: ctx: 32 (over z, y, x, core).
Axes of the slice: x: 2, y: 2, z: 4, core: 2. Of those that a mesh axis runs over, the one named last changes fastest.
Arguments:
- queries: bfloat16 [32768, 2048], P('ctx'), may hold values from -6 to 6
- keys: bfloat16 [32768, 2048], P('ctx'), may hold values from -6 to 6
- values: bfloat16 [32768, 2048], P('ctx'), may hold values from -6 to 6
- level_gate: bfloat16 [32768, 128], P('ctx'), may hold values from 0.19921875 to 2
- norm_gain: float32 [2048], replicated, may hold values from 0.5 to 1.5
- out_weight: bfloat16 [2048, 2048], P('ctx'), may hold values from -0.125 to 0.125
Outputs:
- layer_out: bfloat16 [32768, 2048], P('ctx')
The draws below stay inside these ranges and needn't reach their ends.
All inputs are finite; a program needn't handle non-finite values.
Results may differ from the reference program's by a relative error of at most 0.0057.
Values may be sent and summed in bfloat16 or wider, within the bound.
A program may use at most 192 MiB of HBM per device.

```python
import math
import jax
import jax.numpy as jnp
from jax import lax

HEADS = 16
HEAD = 128
D = 2048
TOK_DEV = 1024
GATES = 8
TOKENS = 32768
N_CTX = 32


def block_levels(rng, dims, split, smallest, top_value):
    def one(dim, blocks):
        draws = jax.random.uniform(jax.random.fold_in(jax.random.fold_in(rng, 6), dim), (blocks,), jnp.float32, smallest / len(split), top_value / len(split))
        return jnp.repeat(jnp.exp(draws), dims[dim] // blocks).reshape((-1,) + (1,) * (len(dims) - dim - 1))

    loudness = one(*split[0])
    for cut in split[1:]:
        loudness = loudness * one(*cut)
    return loudness


def normal_values(key, dims, width, most, split=(), held_as=jnp.bfloat16):
    result = width * jax.random.normal(key, dims, jnp.float32)
    if split:
        result = result * block_levels(key, dims, split, -0.22, 0.18)
    return jnp.clip(result, -most, most).astype(held_as)


def setup_inputs(seed: int = 0) -> dict:
    seeds = jax.random.split(jax.random.key(seed), 7)
    queries = normal_values(seeds[0], (TOKENS, D), 1.0, 6.0, ((0, 32),))
    keys = normal_values(seeds[1], (TOKENS, D), 1.0, 6.0, ((0, 32),))
    values = normal_values(seeds[2], (TOKENS, D), 1.0, 6.0, ((0, 32),))
    level_gate = jnp.clip(jnp.exp(math.log(2.0) - 2.306499 * jax.random.uniform(seeds[3], (TOKENS, GATES * HEADS), jnp.float32) ** block_levels(seeds[3], (TOKENS, GATES * HEADS), ((0, 32),), -0.2, 0.2)), 0.19921875, 2.0).astype(jnp.bfloat16)
    norm_gain = jnp.clip(1.0 + 0.1 * jax.random.normal(seeds[4], (D,), jnp.float32), 0.5, 1.5)
    out_weight = normal_values(seeds[5], (D, D), D ** -0.5, 0.125, ((0, 32),))
    return dict(queries=queries, keys=keys, values=values, level_gate=level_gate, norm_gain=norm_gain, out_weight=out_weight)


EPSILON = 1e-06
HIGH = lax.Precision.HIGHEST

def within_shard(query_heads, key_heads, value_heads, level_weights):
    scores = jnp.einsum('thd,shd->hts', query_heads.astype(jnp.float32), key_heads.astype(jnp.float32), precision=HIGH)
    positions = jnp.arange(query_heads.shape[0], dtype=jnp.int32)
    causal = positions[:, None] >= positions[None, :]
    weighted = jnp.where(causal[None], scores, jnp.float32(0.0)).astype(jnp.bfloat16)
    mixed = jnp.einsum('hts,shd->thd', weighted.astype(jnp.float32), value_heads.astype(jnp.float32), precision=HIGH)
    return mixed * level_weights[:, 0, :, None]

def finish(summed, norm_gain):
    squares = lax.optimization_barrier(jnp.mean(summed * summed, axis=-1, keepdims=True))
    normed = summed * lax.rsqrt(squares + EPSILON) * norm_gain.reshape(HEADS, HEAD)
    return normed.reshape(summed.shape[0], HEADS * HEAD).astype(jnp.bfloat16)

def reference(queries, keys, values, level_gate, norm_gain, out_weight):
    shards = N_CTX
    levels = shards.bit_length() - 1
    query_all = queries.reshape(shards, TOK_DEV, HEADS, HEAD)
    key_all = keys.reshape(shards, TOK_DEV, HEADS, HEAD)
    value_all = values.reshape(shards, TOK_DEV, HEADS, HEAD)
    weight_all = level_gate.reshape(shards, TOK_DEV, GATES, HEADS).astype(jnp.float32)

    def shard_state(pair):
        return jnp.einsum('shd,she->hde', pair[0].astype(jnp.float32), pair[1].astype(jnp.float32), precision=HIGH)
    states = lax.map(shard_state, (key_all, value_all))
    tables = [states.reshape(shards >> level_index, 1 << level_index, HEADS, HEAD, HEAD).sum(1) for level_index in range(levels)]

    def one_shard(position):
        query_heads = query_all[position]
        level_weights = weight_all[position]
        summed = within_shard(query_heads, key_all[position], value_all[position], level_weights)
        for level_index in range(levels):
            upper_half = position >> level_index & 1 == 1
            block = jnp.maximum((position >> level_index) - 1, 0)
            bucket = jnp.where(upper_half, tables[level_index][block], jnp.float32(0.0)).astype(jnp.bfloat16)
            product = jnp.einsum('thd,hde->the', query_heads.astype(jnp.float32), bucket.astype(jnp.float32), precision=HIGH)
            summed = summed + level_weights[:, level_index + 1, :, None] * product
        return finish(summed, norm_gain)
    mixed = lax.map(one_shard, jnp.arange(shards, dtype=jnp.int32))
    mixed = mixed.reshape(shards * TOK_DEV, HEADS * HEAD)
    return jnp.dot(mixed, out_weight, preferred_element_type=jnp.float32).astype(jnp.bfloat16)
```

```python
import functools
import jax
import jax.numpy as jnp
from jax import lax
from jax.experimental import pallas as pl
from jax.experimental.pallas import tpu as pltpu
from jax.sharding import PartitionSpec as P

HEAD = 128
CHUNK = 256
EPSILON = 1e-06
F32 = jnp.float32
BF16 = jnp.bfloat16


def dot(a, b, dims):
    return lax.dot_general(a, b, (dims, ((), ())), preferred_element_type=F32)


def states_kernel(heads, chunks, k_ref, v_ref, prefix_ref, total_ref):
    for h in range(heads):
        cols = slice(h * HEAD, (h + 1) * HEAD)
        running = None
        for c in range(chunks):
            rows = slice(c * CHUNK, (c + 1) * CHUNK)
            one = dot(k_ref[rows, cols], v_ref[rows, cols], ((0,), (0,)))
            prefix_ref[c, h] = (jnp.zeros_like(one) if running is None else running).astype(BF16)
            running = one if running is None else running + one
        total_ref[h] = running


def chunk_states(keys, values):
    rows, width = keys.shape
    heads, chunks = width // HEAD, rows // CHUNK
    per = 4
    while heads % per:
        per //= 2
    return pl.pallas_call(
        functools.partial(states_kernel, per, chunks),
        grid=(heads // per,),
        in_specs=[pl.BlockSpec((rows, per * HEAD), lambda i: (0, i))] * 2,
        out_specs=[
            pl.BlockSpec((chunks, per, HEAD, HEAD), lambda i: (0, i, 0, 0)),
            pl.BlockSpec((per, HEAD, HEAD), lambda i: (i, 0, 0)),
        ],
        out_shape=[
            jax.ShapeDtypeStruct((chunks, heads, HEAD, HEAD), BF16),
            jax.ShapeDtypeStruct((heads, HEAD, HEAD), F32),
        ],
        cost_estimate=pl.CostEstimate(flops=2 * rows * width * HEAD, bytes_accessed=4 * rows * width, transcendentals=0),
        name="states",
    )(keys, values)


def local_kernel(heads, q_ref, k_ref, v_ref, gate_ref, prefix_ref, out_ref):
    gate = gate_ref[...].astype(F32)
    rows = lax.broadcasted_iota(jnp.int32, (CHUNK, CHUNK), 0)
    cols = lax.broadcasted_iota(jnp.int32, (CHUNK, CHUNK), 1)
    causal = rows >= cols
    for h in range(heads):
        at = slice(h * HEAD, (h + 1) * HEAD)
        q = q_ref[:, at]
        scores = dot(q, k_ref[:, at], ((1,), (1,)))
        scores = jnp.where(causal, scores, 0.0).astype(BF16)
        mixed = dot(scores, v_ref[:, at], ((1,), (0,))) + dot(q, prefix_ref[0, h], ((1,), (0,)))
        out_ref[:, at] = mixed * gate[:, h : h + 1]


def local_term(queries, keys, values, gate, prefix):
    rows, width = queries.shape
    heads, chunks = width // HEAD, rows // CHUNK
    row_block = pl.BlockSpec((CHUNK, width), lambda i: (i, 0))
    return pl.pallas_call(
        functools.partial(local_kernel, heads),
        grid=(chunks,),
        in_specs=[
            row_block,
            row_block,
            row_block,
            pl.BlockSpec((CHUNK, gate.shape[1]), lambda i: (i, 0)),
            pl.BlockSpec((1, heads, HEAD, HEAD), lambda i: (i, 0, 0, 0)),
        ],
        out_specs=row_block,
        out_shape=jax.ShapeDtypeStruct((rows, width), F32),
        cost_estimate=pl.CostEstimate(flops=10 * rows * width * CHUNK, bytes_accessed=10 * rows * width, transcendentals=0),
        name="local",
    )(queries, keys, values, gate, prefix)


def finish_kernel(heads, levels, q_ref, local_ref, gate_ref, gain_ref, bucket_ref, w_ref, out_ref, normed_ref):
    gate = gate_ref[...].astype(F32)
    for h in range(heads):
        at = slice(h * HEAD, (h + 1) * HEAD)
        product = dot(q_ref[:, at], bucket_ref[h], ((1,), (0,)))
        total = local_ref[:, at]
        for level in range(levels):
            lane = (level + 1) * heads + h
            total = total + gate[:, lane : lane + 1] * product[:, level * HEAD : (level + 1) * HEAD]
        squares = jnp.mean(total * total, axis=-1, keepdims=True)
        normed = total * lax.rsqrt(squares + EPSILON) * gain_ref[:, at]
        normed_ref[:, at] = normed.astype(BF16)
    out_ref[...] = jnp.dot(normed_ref[...], w_ref[...], preferred_element_type=F32).astype(BF16)


def finish(queries, local, gate, gain, buckets, weight):
    rows, width = queries.shape
    heads = width // HEAD
    levels = buckets.shape[2] // HEAD
    out_width = weight.shape[1]
    row_block = pl.BlockSpec((CHUNK, width), lambda i: (i, 0))
    once = pl.Buffered(1)
    return pl.pallas_call(
        functools.partial(finish_kernel, heads, levels),
        grid=(rows // CHUNK,),
        in_specs=[
            row_block,
            row_block,
            pl.BlockSpec((CHUNK, gate.shape[1]), lambda i: (i, 0)),
            pl.BlockSpec((1, width), lambda i: (0, 0)),
            pl.BlockSpec(buckets.shape, lambda i: (0, 0, 0), pipeline_mode=once),
            pl.BlockSpec(weight.shape, lambda i: (0, 0), pipeline_mode=once),
        ],
        out_specs=pl.BlockSpec((CHUNK, out_width), lambda i: (i, 0)),
        out_shape=jax.ShapeDtypeStruct((rows, out_width), BF16),
        scratch_shapes=[pltpu.VMEM((CHUNK, width), BF16)],
        cost_estimate=pl.CostEstimate(flops=4 * rows * width * out_width, bytes_accessed=20 * rows * width, transcendentals=0),
        name="finish",
    )(queries, local, gate, gain, buckets, weight)


def exchange(value, axis, bit):
    pairs = [(source, source ^ 2**bit) for source in range(lax.axis_size(axis))]
    return lax.ppermute(value, axis, pairs)


def shards(queries, keys, values, level_gate, norm_gain, out_weight):
    heads = queries.shape[1] // HEAD
    half = heads // 2
    position = lax.axis_index("ctx")
    levels = lax.axis_size("ctx").bit_length() - 1
    whole_weight = lax.all_gather(out_weight, "ctx", axis=0, tiled=True)
    prefix, total = chunk_states(keys, values)
    odd = position & 1 == 1
    from_pair = exchange(total.astype(BF16), "ctx", 0)
    first = jnp.where(odd, from_pair, jnp.zeros_like(from_pair))
    both = total + from_pair.astype(F32)
    running = jnp.where(odd, both[half:], both[:half])
    mine = []
    for level in range(1, levels):
        partner = exchange(running.astype(BF16), "ctx", level)
        upper = position >> level & 1 == 1
        mine.append(jnp.where(upper, partner, jnp.zeros_like(partner)))
        running = running + partner.astype(F32)
    mine = jnp.stack(mine, 0)
    other = exchange(mine, "ctx", 0)
    low = jnp.where(odd, other, mine)
    high = jnp.where(odd, mine, other)
    rest = jnp.concatenate([low, high], 1)
    buckets = jnp.concatenate([first[None], rest], 0)
    buckets = buckets.transpose(1, 2, 0, 3).reshape(heads, HEAD, levels * HEAD)
    local = local_term(queries, keys, values, level_gate, prefix)
    return finish(queries, local, level_gate, norm_gain.reshape(1, -1), buckets, whole_weight)


def solution(mesh):
    placed = (P("ctx", None), P("ctx", None), P("ctx", None), P("ctx", None), P(), P("ctx", None))
    return jax.shard_map(
        shards, mesh=mesh, in_specs=placed, out_specs=P("ctx", None), check_vma=False
    )
```

```python
import functools
import jax
import jax.numpy as jnp
from jax import lax
from jax.experimental import pallas as pl
from jax.experimental.pallas import tpu as pltpu
from jax.sharding import PartitionSpec as P

HEAD = 128
CHUNK = 256
EPSILON = 1e-06
F32 = jnp.float32
BF16 = jnp.bfloat16
MESH = pl.DeviceIdType.MESH


def dot(a, b, dims):
    return lax.dot_general(a, b, (dims, ((), ())), preferred_element_type=F32)


def other(me, mask):
    bit = 1
    out = me
    while bit <= mask:
        if mask & bit:
            out = out + bit * (1 - 2 * ((me // bit) % 2))
        bit *= 2
    return out


def transfers(levels, columns):
    names = [("stage", l) for l in range(levels)] + [("pass", l) for l in range(1, levels)]
    names += [("z", j) for j in range(1, columns)]
    for kind in ("x", "y", "dx", "dy", "c0", "c2", "c4", "c6"):
        names += [(kind, j) for j in range(columns)]
    return {name: at for at, name in enumerate(names)}


def kernel(n, q_hbm, k_hbm, v_hbm, gate_ref, gain_ref, w_ref, out_hbm,
           q, k, v, whole, acc, prefix, total, running, buckets, first, sends, load_sem, send_sem, recv_sem):
    rows, width = q.shape
    heads, chunks = width // HEAD, rows // CHUNK
    half = heads // 2
    levels = n.bit_length() - 1
    columns = n // 8
    part = w_ref.shape[0]
    ids = transfers(levels, columns)
    me = lax.axis_index("ctx")
    core = me % 2
    mine = pl.ds(core * half, half)
    yours = pl.ds((1 - core) * half, half)

    def load(hbm, buffer, kind, c):
        at = pl.ds(c * CHUNK, CHUNK)
        return pltpu.make_async_copy(hbm.at[at], buffer.at[at], load_sem.at[kind, c])

    for c in range(chunks):
        load(k_hbm, k, 0, c).start()
        load(v_hbm, v, 1, c).start()
    for c in range(chunks):
        load(q_hbm, q, 2, c).start()

    masks = sorted({1 << l for l in range(levels)} | {j << 3 for j in range(1, columns)})
    barrier = pltpu.get_barrier_semaphore()
    for mask in masks:
        pl.semaphore_signal(barrier, inc=1, device_id=(other(me, mask),), device_id_type=MESH)
    pl.semaphore_wait(barrier, len(masks))

    def copy(name, src, dst, mask):
        at = ids[name]
        return pltpu.make_async_remote_copy(
            src_ref=src, dst_ref=dst, send_sem=send_sem.at[at], recv_sem=recv_sem.at[at],
            device_id=(other(me, mask),), device_id_type=MESH,
        )

    def shard(mask, side=None):
        at = pl.ds(pl.multiple_of(other(me, mask) * part, part), part)
        if side is None:
            return whole.at[at]
        width_here = whole.shape[1] // 2
        return whole.at[at, pl.ds(side * width_here, width_here)]

    def send(name):
        kind, j = name
        if kind == "stage":
            if j == 0:
                return copy(name, first, buckets.at[0], 1)
            return copy(name, sends.at[j - 1], buckets.at[j, mine], 1 << j)
        if kind == "pass":
            return copy(name, buckets.at[j, mine], buckets.at[j, mine], 1)
        col = j << 3
        if kind == "z":
            return copy(name, w_ref, shard(0), col)
        if kind in ("x", "y", "c0"):
            mask = {"x": 2, "y": 4, "c0": 1}[kind]
            return copy(name, w_ref if j == 0 else shard(col), shard(col), mask)
        if kind == "dy":
            return copy(name, shard(2 ^ col, 0), shard(2 ^ col, 0), 4)
        if kind == "dx":
            return copy(name, shard(4 ^ col, 1), shard(4 ^ col, 1), 2)
        group = int(kind[1])
        return copy(name, shard(group ^ col), shard(group ^ col), 1)

    def arrival(name):
        kind, j = name
        if kind == "stage":
            dst, mask = (buckets.at[0], 1) if j == 0 else (buckets.at[j, mine], 1 << j)
        elif kind == "pass":
            dst, mask = buckets.at[j, yours], 1
        else:
            col = j << 3
            if kind == "z":
                dst, mask = shard(col), col
            elif kind in ("x", "y"):
                mask = {"x": 2, "y": 4}[kind]
                dst = shard(mask ^ col)
            elif kind == "dy":
                dst, mask = shard(6 ^ col, 0), 4
            elif kind == "dx":
                dst, mask = shard(6 ^ col, 1), 2
            else:
                dst, mask = shard(1 ^ int(kind[1]) ^ col), 1
        return copy(name, dst, dst, mask)

    def start(*name):
        send(name).start()

    def receive(*name):
        arrival(name).wait_recv()

    own = pltpu.make_async_copy(w_ref, shard(0), load_sem.at[3, 0])
    own.start()
    for j in range(1, columns):
        start("z", j)
    start("x", 0)
    start("y", 0)
    start("c0", 0)

    total[...] = jnp.zeros_like(total)

    def state_step(c, carry):
        load(k_hbm, k, 0, c).wait()
        load(v_hbm, v, 1, c).wait()
        at = pl.ds(pl.multiple_of(c * CHUNK, CHUNK), CHUNK)
        for h in range(heads):
            cols = slice(h * HEAD, (h + 1) * HEAD)
            before = total[h]
            prefix[c, h] = before.astype(BF16)
            total[h] = before + dot(k[at, cols], v[at, cols], ((0,), (0,)))
        return carry

    lax.fori_loop(0, chunks, state_step, 0)
    first[...] = total[...].astype(BF16)
    start("stage", 0)

    def advance(l):
        receive("stage", l)
        if l == 0:
            running[...] = total[mine] + buckets[0, mine].astype(F32)
        elif l + 1 < levels:
            running[...] = running[...] + buckets[l, mine].astype(F32)
        if l + 1 < levels:
            sends[l] = running[...].astype(BF16)
            start("stage", l + 1)
        if l > 0:
            start("pass", l)

    def column_arrived(j):
        receive("z", j)
        for kind in ("x", "y", "c0"):
            start(kind, j)

    def sides_arrived(j):
        receive("x", j)
        start("dy", j)
        receive("y", j)
        start("dx", j)
        start("c2", j)
        start("c4", j)

    def local_step(c, carry):
        load(q_hbm, q, 2, c).wait()
        at = pl.ds(pl.multiple_of(c * CHUNK, CHUNK), CHUNK)
        gate = gate_ref[at, :].astype(F32)
        causal = lax.broadcasted_iota(jnp.int32, (CHUNK, CHUNK), 0) >= lax.broadcasted_iota(
            jnp.int32, (CHUNK, CHUNK), 1
        )
        for h in range(heads):
            cols = slice(h * HEAD, (h + 1) * HEAD)
            query = q[at, cols]
            scores = dot(query, k[at, cols], ((1,), (1,)))
            scores = jnp.where(causal, scores, 0.0).astype(BF16)
            mixed = dot(scores, v[at, cols], ((1,), (0,))) + dot(query, prefix[c, h], ((1,), (0,)))
            acc[at, cols] = mixed * gate[:, h : h + 1]
        for step in range(chunks):
            @pl.when(c == step)
            def _():
                for l in range(levels - 1):
                    if min(l, chunks - 1) == step:
                        advance(l)
                for j in range(1, columns):
                    if min(j - 1, chunks - 1) == step:
                        column_arrived(j)
        return carry

    lax.fori_loop(0, chunks, local_step, 0)

    flags = [((me // (1 << l)) % 2).astype(F32) for l in range(levels)]

    for l in range(1, levels - 1):
        receive("pass", l)

    def early_step(c, carry):
        at = pl.ds(pl.multiple_of(c * CHUNK, CHUNK), CHUNK)
        gate = gate_ref[at, :].astype(F32)
        scaled = [gate[:, (l + 1) * heads : (l + 2) * heads] * flags[l] for l in range(levels - 1)]
        for h in range(heads):
            cols = slice(h * HEAD, (h + 1) * HEAD)
            query = q[at, cols]
            joined = jnp.concatenate([buckets[l, h] for l in range(levels - 1)], axis=1)
            product = dot(query, joined, ((1,), (0,)))
            sofar = acc[at, cols]
            for l in range(levels - 1):
                sofar = sofar + scaled[l][:, h : h + 1] * product[:, l * HEAD : (l + 1) * HEAD]
            acc[at, cols] = sofar
        for step in range(chunks):
            @pl.when(c == step)
            def _():
                for j in range(columns):
                    if min(j, chunks - 1) == step:
                        sides_arrived(j)
        return carry

    lax.fori_loop(0, chunks, early_step, 0)
    advance(levels - 1)
    receive("pass", levels - 1)

    def last_step(c, carry):
        at = pl.ds(pl.multiple_of(c * CHUNK, CHUNK), CHUNK)
        top = levels - 1
        scaled = gate_ref[at, (top + 1) * heads : (top + 2) * heads].astype(F32) * flags[top]
        for h in range(heads):
            cols = slice(h * HEAD, (h + 1) * HEAD)
            product = dot(q[at, cols], buckets[top, h], ((1,), (0,)))
            attended = acc[at, cols] + scaled[:, h : h + 1] * product
            squares = jnp.mean(attended * attended, axis=-1, keepdims=True)
            normed = attended * lax.rsqrt(squares + EPSILON) * gain_ref[:, cols]
            k[at, cols] = normed.astype(BF16)
        for step in range(chunks):
            @pl.when(c == step)
            def _():
                for j in range(columns):
                    if min(j, chunks - 1) == step:
                        receive("dy", j)
                        receive("dx", j)
                        start("c6", j)
        return carry

    lax.fori_loop(0, chunks, last_step, 0)
    own.wait()
    for kind in ("c0", "c2", "c4", "c6"):
        for j in range(columns):
            receive(kind, j)

    def store(c):
        at = pl.ds(pl.multiple_of(c * CHUNK, CHUNK), CHUNK)
        return pltpu.make_async_copy(v.at[at], out_hbm.at[at], load_sem.at[4, c])

    def project_step(c, carry):
        at = pl.ds(pl.multiple_of(c * CHUNK, CHUNK), CHUNK)
        v[at, :] = jnp.dot(k[at, :], whole[...], preferred_element_type=F32).astype(BF16)
        store(c).start()
        return carry

    lax.fori_loop(0, chunks, project_step, 0)
    for name in ids:
        send(name).wait_send()
    for c in range(chunks):
        store(c).wait()


def shards(queries, keys, values, level_gate, norm_gain, out_weight):
    n = lax.axis_size("ctx")
    rows, width = queries.shape
    heads, chunks = width // HEAD, rows // CHUNK
    levels = n.bit_length() - 1
    count = len(transfers(levels, n // 8))
    vmem = pl.BlockSpec(memory_space=pltpu.VMEM)
    hbm = pl.BlockSpec(memory_space=pl.ANY)
    return pl.pallas_call(
        functools.partial(kernel, n),
        out_shape=jax.ShapeDtypeStruct((rows, out_weight.shape[1]), BF16),
        in_specs=[hbm, hbm, hbm, vmem, vmem, vmem],
        out_specs=hbm,
        scratch_shapes=[
            pltpu.VMEM((rows, width), BF16),
            pltpu.VMEM((rows, width), BF16),
            pltpu.VMEM((rows, width), BF16),
            pltpu.VMEM((n * out_weight.shape[0], out_weight.shape[1]), BF16),
            pltpu.VMEM((rows, width), F32),
            pltpu.VMEM((chunks, heads, HEAD, HEAD), BF16),
            pltpu.VMEM((heads, HEAD, HEAD), F32),
            pltpu.VMEM((heads // 2, HEAD, HEAD), F32),
            pltpu.VMEM((levels, heads, HEAD, HEAD), BF16),
            pltpu.VMEM((heads, HEAD, HEAD), BF16),
            pltpu.VMEM((levels - 1, heads // 2, HEAD, HEAD), BF16),
            pltpu.SemaphoreType.DMA((5, chunks)),
            pltpu.SemaphoreType.DMA((count,)),
            pltpu.SemaphoreType.DMA((count,)),
        ],
        compiler_params=pltpu.CompilerParams(
            collective_id=0, has_side_effects=True, vmem_limit_bytes=60 * 1024 * 1024
        ),
        name="layer",
    )(queries, keys, values, level_gate, norm_gain.reshape(1, -1), out_weight)


def solution(mesh):
    placed = (P("ctx", None), P("ctx", None), P("ctx", None), P("ctx", None), P(), P("ctx", None))
    return jax.shard_map(
        shards, mesh=mesh, in_specs=placed, out_specs=P("ctx", None), check_vma=False
    )
```

```python
import functools
import jax
import jax.numpy as jnp
from jax import lax
from jax.experimental import pallas as pl
from jax.experimental.pallas import tpu as pltpu
from jax.sharding import PartitionSpec as P

HEAD = 128
CHUNK = 256
EPSILON = 1e-06
F32 = jnp.float32
BF16 = jnp.bfloat16
MESH = pl.DeviceIdType.MESH


def dot(a, b, dims):
    return lax.dot_general(a, b, (dims, ((), ())), preferred_element_type=F32)


def other(me, mask):
    bit = 1
    out = me
    while bit <= mask:
        if mask & bit:
            out = out + bit * (1 - 2 * ((me // bit) % 2))
        bit *= 2
    return out


def transfers(levels, columns):
    names = [("stage", 0)]
    for l in range(1, levels):
        names += [(kind, l, g) for kind in ("stage", "pass") for g in range(2)]
    names += [("z", j) for j in range(1, columns)]
    for kind in ("x", "y", "dx", "dy", "c0", "c2", "c4", "c6"):
        names += [(kind, j) for j in range(columns)]
    return {name: at for at, name in enumerate(names)}


def plane_rows(me, column, part):
    first_row = other(me, column << 3) // 8 * (8 * part)
    return pl.ds(pl.multiple_of(first_row, 8 * part), 8 * part)


def kernel(n, q_hbm, k_hbm, v_hbm, gate_ref, gain_ref, w_ref, acc, k, whole,
           q, v, prefix, total, running, buckets, first, sends, load_sem, send_sem, recv_sem):
    rows, width = q.shape
    heads, chunks = width // HEAD, rows // CHUNK
    half = heads // 2
    levels = n.bit_length() - 1
    columns = n // 8
    part = w_ref.shape[0]
    ids = transfers(levels, columns)
    me = lax.axis_index("ctx")
    core = me % 2
    group = half // 2

    def part_of(core_bit, g):
        return pl.ds(core_bit * half + g * group, group)


    def load(hbm, buffer, kind, c):
        at = pl.ds(c * CHUNK, CHUNK)
        return pltpu.make_async_copy(hbm.at[at], buffer.at[at], load_sem.at[kind, c])

    for c in range(chunks):
        load(k_hbm, k, 0, c).start()
        load(v_hbm, v, 1, c).start()
    for c in range(chunks):
        load(q_hbm, q, 2, c).start()

    masks = sorted({1 << l for l in range(levels)} | {j << 3 for j in range(1, columns)})
    barrier = pltpu.get_barrier_semaphore()
    for mask in masks:
        pl.semaphore_signal(barrier, inc=1, device_id=(other(me, mask),), device_id_type=MESH)
    pl.semaphore_wait(barrier, len(masks))

    def copy(name, src, dst, mask):
        at = ids[name]
        return pltpu.make_async_remote_copy(
            src_ref=src, dst_ref=dst, send_sem=send_sem.at[at], recv_sem=recv_sem.at[at],
            device_id=(other(me, mask),), device_id_type=MESH,
        )

    def shard(mask, side=None):
        at = pl.ds(pl.multiple_of(other(me, mask) * part, part), part)
        if side is None:
            return whole.at[at]
        width_here = whole.shape[1] // 2
        return whole.at[at, pl.ds(side * width_here, width_here)]

    def send(name):
        kind, j = name[:2]
        if kind == "stage" and j == 0:
            return copy(name, first, buckets.at[0], 1)
        if kind in ("stage", "pass"):
            here = buckets.at[j, part_of(core, name[2])]
            if kind == "stage":
                return copy(name, sends.at[j - 1, pl.ds(name[2] * group, group)], here, 1 << j)
            return copy(name, here, here, 1)
        col = j << 3
        if kind == "z":
            low = j & -j
            if low == j:
                return copy(name, w_ref, shard(0), col)
            return copy(name, shard((j ^ low) << 3), shard((j ^ low) << 3), low << 3)
        if kind in ("x", "y", "c0"):
            mask = {"x": 2, "y": 4, "c0": 1}[kind]
            return copy(name, w_ref if j == 0 else shard(col), shard(col), mask)
        if kind == "dy":
            return copy(name, shard(2 ^ col, 0), shard(2 ^ col, 0), 4)
        if kind == "dx":
            return copy(name, shard(4 ^ col, 1), shard(4 ^ col, 1), 2)
        block = int(kind[1])
        return copy(name, shard(block ^ col), shard(block ^ col), 1)

    def arrival(name):
        kind, j = name[:2]
        if kind == "stage" and j == 0:
            dst, mask = buckets.at[0], 1
        elif kind == "stage":
            dst, mask = buckets.at[j, part_of(core, name[2])], 1 << j
        elif kind == "pass":
            dst, mask = buckets.at[j, part_of(1 - core, name[2])], 1
        else:
            col = j << 3
            if kind == "z":
                dst, mask = shard(col), (j & -j) << 3
            elif kind in ("x", "y"):
                mask = {"x": 2, "y": 4}[kind]
                dst = shard(mask ^ col)
            elif kind == "dy":
                dst, mask = shard(6 ^ col, 0), 4
            elif kind == "dx":
                dst, mask = shard(6 ^ col, 1), 2
            else:
                dst, mask = shard(1 ^ int(kind[1]) ^ col), 1
        return copy(name, dst, dst, mask)

    def start(*name):
        send(name).start()

    def receive(*name):
        arrival(name).wait_recv()

    own = pltpu.make_async_copy(w_ref, shard(0), load_sem.at[3, 0])
    own.start()
    for l in range(3, levels):
        start("z", 1 << (l - 3))
    start("x", 0)
    start("y", 0)
    start("c0", 0)

    total[...] = jnp.zeros_like(total)

    def state_step(c, carry):
        load(k_hbm, k, 0, c).wait()
        load(v_hbm, v, 1, c).wait()
        at = pl.ds(pl.multiple_of(c * CHUNK, CHUNK), CHUNK)
        for h in range(heads):
            cols = slice(h * HEAD, (h + 1) * HEAD)
            before = total[h]
            prefix[c, h] = before.astype(BF16)
            total[h] = before + dot(k[at, cols], v[at, cols], ((0,), (0,)))
        return carry

    lax.fori_loop(0, chunks, state_step, 0)
    first[...] = total[...].astype(BF16)
    start("stage", 0)

    def send_on(l, g):
        at = pl.ds(g * group, group)
        sends[l, at] = running[at].astype(BF16)
        start("stage", l + 1, g)

    def advance(l, g):
        receive("stage", l, g)
        if l + 1 < levels:
            at = pl.ds(g * group, group)
            running[at] = running[at] + buckets[l, part_of(core, g)].astype(F32)
            send_on(l, g)
        start("pass", l, g)

    def advance_first():
        receive("stage", 0)
        at = pl.ds(core * half, half)
        running[...] = total[at] + buckets[0, at].astype(F32)
        for g in range(2):
            send_on(0, g)

    def column_arrived(j, kinds):
        receive("z", j)
        bit = 1
        while bit < (j & -j):
            start("z", j | bit)
            bit *= 2
        for kind in kinds:
            start(kind, j)

    def sides_arrived(j):
        receive("x", j)
        start("dy", j)
        receive("y", j)
        start("dx", j)
        start("c2", j)
        start("c4", j)

    def local_step(c, carry):
        load(q_hbm, q, 2, c).wait()
        at = pl.ds(pl.multiple_of(c * CHUNK, CHUNK), CHUNK)
        gate = gate_ref[at, :].astype(F32)
        causal = lax.broadcasted_iota(jnp.int32, (CHUNK, CHUNK), 0) >= lax.broadcasted_iota(
            jnp.int32, (CHUNK, CHUNK), 1
        )
        for h in range(heads):
            cols = slice(h * HEAD, (h + 1) * HEAD)
            query = q[at, cols]
            scores = dot(query, k[at, cols], ((1,), (1,)))
            scores = jnp.where(causal, scores, 0.0).astype(BF16)
            mixed = dot(scores, v[at, cols], ((1,), (0,))) + dot(query, prefix[c, h], ((1,), (0,)))
            acc[at, cols] = mixed * gate[:, h : h + 1]
            between(c, h, local_tasks)
        return carry

    def between(c, h, tasks):
        if (h + 1) % half:
            return
        for point, task in tasks.items():
            if point % 2 == h // half:
                pl.when(c == point // 2)(task)

    def task_after_first():
        advance_first()
        start("x", 1)

    def task_last_local():
        advance(1, 1)
        start("x", 2)
        start("y", 2)

    local_tasks = {
        0: task_after_first,
        3: lambda: column_arrived(2, ("c0",)),
        4: lambda: advance(1, 0),
        7: task_last_local,
    }
    column_arrived(1, ("y", "c0"))
    lax.fori_loop(0, chunks, local_step, 0)
    advance(2, 0)
    for j in range(3, columns):
        column_arrived(j, ("x", "y", "c0"))
    advance(2, 1)
    sides_arrived(0)
    for l in range(3, levels - 1):
        for g in range(2):
            advance(l, g)

    flags = [((me // (1 << l)) % 2).astype(F32) for l in range(levels)]

    for l in range(1, levels - 1):
        for g in range(2):
            receive("pass", l, g)

    def early_step(c, carry):
        at = pl.ds(pl.multiple_of(c * CHUNK, CHUNK), CHUNK)
        gate = gate_ref[at, :].astype(F32)
        scaled = [gate[:, (l + 1) * heads : (l + 2) * heads] * flags[l] for l in range(levels - 1)]
        for h in range(heads):
            cols = slice(h * HEAD, (h + 1) * HEAD)
            query = q[at, cols]
            joined = jnp.concatenate([buckets[l, h] for l in range(levels - 1)], axis=1)
            product = dot(query, joined, ((1,), (0,)))
            sofar = acc[at, cols]
            for l in range(levels - 1):
                sofar = sofar + scaled[l][:, h : h + 1] * product[:, l * HEAD : (l + 1) * HEAD]
            acc[at, cols] = sofar
            between(c, h, early_tasks)
        return carry

    def diagonal_arrived(j):
        receive("dy", j)
        receive("dx", j)
        start("c6", j)

    def task_sides_rest():
        for j in range(3, columns):
            sides_arrived(j)

    early_tasks = {
        0: lambda: sides_arrived(1),
        3: lambda: sides_arrived(2),
        5: lambda: diagonal_arrived(0),
        6: task_sides_rest,
    }
    lax.fori_loop(0, chunks, early_step, 0)
    for g in range(2):
        advance(levels - 1, g)
    for g in range(2):
        receive("pass", levels - 1, g)

    def last_step(c, carry):
        at = pl.ds(pl.multiple_of(c * CHUNK, CHUNK), CHUNK)
        top = levels - 1
        scaled = gate_ref[at, (top + 1) * heads : (top + 2) * heads].astype(F32) * flags[top]
        for h in range(heads):
            cols = slice(h * HEAD, (h + 1) * HEAD)
            product = dot(q[at, cols], buckets[top, h], ((1,), (0,)))
            attended = acc[at, cols] + scaled[:, h : h + 1] * product
            squares = jnp.mean(attended * attended, axis=-1, keepdims=True)
            normed = attended * lax.rsqrt(squares + EPSILON) * gain_ref[:, cols]
            k[at, cols] = normed.astype(BF16)
            between(c, h, last_tasks)
        return carry

    last_tasks = {2: lambda: diagonal_arrived(1), 5: lambda: diagonal_arrived(2)}
    lax.fori_loop(0, chunks, last_step, 0)
    own.wait()

    def column_ready(j):
        for kind in ("c0", "c2", "c4", "c6"):
            receive(kind, j)

    def project(j):
        planes = plane_rows(me, j, part)

        def project_step(c, carry):
            at = pl.ds(pl.multiple_of(c * CHUNK, CHUNK), CHUNK)
            product = jnp.dot(k[at, planes], whole[planes, :], preferred_element_type=F32)
            acc[at, :] = product if j == 0 else acc[at, :] + product
            return carry

        lax.fori_loop(0, chunks, project_step, 0)

    for j in range(columns - 1):
        column_ready(j)
        project(j)
        if j + 3 < columns:
            diagonal_arrived(j + 3)
    column_ready(columns - 1)
    for name in ids:
        send(name).wait_send()


def project_kernel(n, part, acc_ref, normed_ref, whole_ref, out_ref):
    planes = plane_rows(lax.axis_index("ctx"), n // 8 - 1, part)
    at = pl.ds(pl.multiple_of(pl.program_id(0) * CHUNK, CHUNK), CHUNK)
    product = jnp.dot(normed_ref[at, planes], whole_ref[planes, :], preferred_element_type=F32)
    out_ref[...] = (acc_ref[at, :] + product).astype(BF16)


def shards(queries, keys, values, level_gate, norm_gain, out_weight):
    n = lax.axis_size("ctx")
    rows, width = queries.shape
    heads, chunks = width // HEAD, rows // CHUNK
    levels = n.bit_length() - 1
    count = len(transfers(levels, n // 8))
    vmem = pl.BlockSpec(memory_space=pltpu.VMEM)
    hbm = pl.BlockSpec(memory_space=pltpu.HBM)
    out_width = out_weight.shape[1]
    weight_rows = n * out_weight.shape[0]
    acc, normed, whole = pl.pallas_call(
        functools.partial(kernel, n),
        out_shape=[
            pltpu.VMEM((rows, width), F32),
            pltpu.VMEM((rows, width), BF16),
            pltpu.VMEM((weight_rows, out_width), BF16),
        ],
        in_specs=[hbm, hbm, hbm, vmem, vmem, vmem],
        out_specs=[vmem] * 3,
        scratch_shapes=[
            pltpu.VMEM((rows, width), BF16),
            pltpu.VMEM((rows, width), BF16),
            pltpu.VMEM((chunks, heads, HEAD, HEAD), BF16),
            pltpu.VMEM((heads, HEAD, HEAD), F32),
            pltpu.VMEM((heads // 2, HEAD, HEAD), F32),
            pltpu.VMEM((levels, heads, HEAD, HEAD), BF16),
            pltpu.VMEM((heads, HEAD, HEAD), BF16),
            pltpu.VMEM((levels - 1, heads // 2, HEAD, HEAD), BF16),
            pltpu.SemaphoreType.DMA((5, chunks)),
            pltpu.SemaphoreType.DMA((count,)),
            pltpu.SemaphoreType.DMA((count,)),
        ],
        compiler_params=pltpu.CompilerParams(
            collective_id=0, has_side_effects=True, vmem_limit_bytes=38 * 1024 * 1024
        ),
        name="layer",
    )(queries, keys, values, level_gate, norm_gain.reshape(1, -1), out_weight)
    return pl.pallas_call(
        functools.partial(project_kernel, n, out_weight.shape[0]),
        grid=(chunks,),
        out_shape=jax.ShapeDtypeStruct((rows, out_width), BF16),
        in_specs=[vmem] * 3,
        out_specs=pl.BlockSpec((CHUNK, out_width), lambda i: (i, 0)),
        compiler_params=pltpu.CompilerParams(vmem_limit_bytes=12 * 1024 * 1024),
        name="project",
    )(acc, normed, whole)


def solution(mesh):
    placed = (P("ctx", None), P("ctx", None), P("ctx", None), P("ctx", None), P(), P("ctx", None))
    return jax.shard_map(
        shards, mesh=mesh, in_specs=placed, out_specs=P("ctx", None), check_vma=False
    )
```
